128 devices in a mesh: pipe: 16 (over x_hi, z, core), tensor: 4 (over y), dp: 2 (over x_lo).
Axes of the slice: x: 4 (x_hi: 2, x_lo: 2; x = x_hi * 2 + x_lo), y: 4, z: 4, core: 2. Of those that a mesh axis runs over, the one named last changes fastest.
Arguments:
- query_heads: bfloat16 [32, 512, 4096], P(('dp', 'pipe'), None, 'tensor'), parts along dimension 0, may hold values from -5 to 5, as said below
- key_heads: bfloat16 [32, 512, 4096], P(('dp', 'pipe'), None, 'tensor'), parts along dimension 0, may hold values from -5 to 5
- value_heads: bfloat16 [32, 512, 4096], P(('dp', 'pipe'), None, 'tensor'), parts along dimension 0, may hold values from -16 to 16
- segment_ids: int32 [32, 512], P(('dp', 'pipe')), parts along dimension 0, may hold values from 0 to 3, never falling along the last dimension, each value on 1 to 256 neighbouring positions
- section_input: bfloat16 [32, 512, 8192], P(('dp', 'pipe'), 'tensor'), parts along dimension 0, may hold values from -6 to 6
- out_weight: bfloat16 [32, 4096, 8192], P(('dp', 'pipe'), 'tensor'), parts along dimension 0, may hold values from -0.1875 to 0.1875
Outputs:
- received: bfloat16 [32, 512, 8192], P(('dp', 'pipe'), 'tensor'), parts along dimension 0
- evicted: bfloat16 [32, 512, 8192], P(('dp', 'pipe'), 'tensor'), parts along dimension 0
- evicted_scale: float32 [32, 512], P(('dp', 'pipe'), 'tensor'), parts along dimension 0
The draws below stay inside these ranges and needn't reach their ends.
There are 2 independent parts, one for each index of `dp`. The reference program is written for one: setup_inputs(seed, part) draws one part's arguments, and reference() takes and returns one part's arrays. A program takes and returns all parts, laid end to end along the dimension named above; each array names one. Nothing has to cross between parts.
Inputs may be any that keep to these rules, and one draw needn't show every extreme that they name: `query_heads`: queries and keys are bfloat16 values of moderate size. `segment_ids`: each section's segment numbers never fall along the tokens; every document is 1 to 256 tokens long.
All inputs are finite; a program needn't handle non-finite values. Where the reference program divides by a largest or mean magnitude, that divisor is 1e-20 or more.
Results may differ from the reference program's by a relative error of at most 0.0055.
Values may be sent and summed in bfloat16 or wider, within the bound.
A program may use at most 128 MiB of HBM per device.

```python
import math
import jax
import jax.numpy as jnp
import numpy as np
from jax import lax

D = 8192
HEADS = 32
HD = 128
ROWS = 512
SECTIONS = 16


def shared_draw(key):
    base_key = jax.random.fold_in(key, 7311)
    query_key, key_key = jax.random.split(base_key, 2)
    shape = (SECTIONS, ROWS, HEADS * HD)
    query_base = jnp.clip(jax.random.normal(query_key, shape, jnp.float32), -4.0, 4.0)
    key_base = jnp.clip(jax.random.normal(key_key, shape, jnp.float32), -4.0, 4.0)
    return (query_base, key_base)


def draw_query_heads(key, part):
    return shared_draw(key)[0].astype(jnp.bfloat16)


def draw_key_heads(key, part):
    return shared_draw(key)[1].astype(jnp.bfloat16)


def level_of(own_key, shape, cuts, low, high):
    def one(dim, blocks):
        draws = jax.random.uniform(jax.random.fold_in(jax.random.fold_in(own_key, 6), dim), (blocks,), jnp.float32, low / len(cuts), high / len(cuts))
        return jnp.repeat(jnp.exp(draws), shape[dim] // blocks).reshape((-1,) + (1,) * (len(shape) - dim - 1))

    level = one(*cuts[0])
    for cut in cuts[1:]:
        level = level * one(*cut)
    return level


def split_up(amount, total, most, skew):
    loads = [(1 << 20) // math.isqrt(rank ** skew) + 1 for rank in range(2, amount + 1)]
    spare, counts = total - most - (amount - 1), [1] * (amount - 1)
    while spare > 0:
        candidates = [i for i in range(amount - 1) if counts[i] < most]
        mass, budget = sum([loads[i] for i in candidates]), spare
        for i in candidates:
            addition = min(most - counts[i], max(1, budget * loads[i] // mass), spare)
            counts[i] = counts[i] + addition
            spare = spare - addition
    return np.array([most] + counts)


def uneven_parts(stream_key, count, total, limit, lean):
    if count == 2:
        one = jax.random.randint(stream_key, (), max(1, total - limit), min(limit, total - 1) + 1)
        return jnp.stack([one, total - one])
    sizes = jnp.asarray(split_up(count, total, limit, lean), jnp.int32)
    pairs = (count - 1) // 2
    donor, sink = sizes[1:1 + 2 * pairs:2], sizes[2:2 + 2 * pairs:2]
    margin = jnp.minimum(donor - 1, limit - sink)
    moved = jax.random.randint(jax.random.fold_in(stream_key, 1), (pairs,), 0, 1 << 20) % (margin + 1)
    sizes = sizes.at[1:1 + 2 * pairs:2].set(donor - moved).at[2:2 + 2 * pairs:2].set(sink + moved)
    return sizes[jax.random.permutation(jax.random.fold_in(stream_key, 2), count)]


def centred(own_key, dims, width, most, cuts=(), kind=jnp.bfloat16):
    loudness = level_of(own_key, dims, cuts, -0.22, 0.18) if cuts else 1.0
    result = jax.random.normal(own_key, dims, jnp.float32) * width * loudness
    return jnp.minimum(jnp.maximum(result, -most), most).astype(kind)


def setup_inputs(seed: int = 0, part: int = 0) -> dict:
    seeds = jax.random.split(jax.random.key(seed), 7)
    own_keys = jax.random.split(jax.random.fold_in(seeds[6], part), 7)
    query_heads = draw_query_heads(jax.random.fold_in(jax.random.fold_in(seeds[6], part), 71), part)
    key_heads = draw_key_heads(jax.random.fold_in(jax.random.fold_in(seeds[6], part), 71), part)
    value_heads = centred(own_keys[2], (SECTIONS, ROWS, HEADS * HD), 4.0, 16.0, ((0, 16), (2, 4)))
    segment_ids = jax.vmap(lambda own: jnp.searchsorted(jnp.cumsum(uneven_parts(own, 4, ROWS, ROWS // 2, 1)), jnp.arange(ROWS), side="right"))(jax.random.split(own_keys[3], SECTIONS)).reshape((SECTIONS, ROWS)).astype(jnp.int32)
    section_input = centred(own_keys[4], (SECTIONS, ROWS, D), 1.0, 6.0, ((0, 16), (1, 4)))
    out_weight = centred(own_keys[5], (SECTIONS, HEADS * HD, D), (HEADS * HD // 4) ** -0.5, 0.1875, ((0, 16), (1, 4)))
    return {"query_heads": query_heads, "key_heads": key_heads, "value_heads": value_heads, "segment_ids": segment_ids, "section_input": section_input, "out_weight": out_weight}


def one_section(operands):
    query_block, key_block, value_block, segment_row, input_block, weight_block = operands
    row_count = query_block.shape[0]
    query_three = query_block.astype(jnp.float32).reshape(row_count, HEADS, HD)
    key_three = key_block.astype(jnp.float32).reshape(row_count, HEADS, HD)
    value_three = value_block.astype(jnp.float32).reshape(row_count, HEADS, HD)
    position = jnp.arange(row_count, dtype=jnp.int32)
    allowed = (segment_row[:, None] == segment_row[None, :]) & (position[None, :] <= position[:, None])
    scores = jnp.einsum('qhd,khd->hqk', query_three, key_three) * (1.0 / math.sqrt(HD))
    scores = jnp.where(allowed[None, :, :], scores, jnp.float32(-1e+30))
    row_max = lax.optimization_barrier(jnp.max(scores, axis=2, keepdims=True))
    expons = jnp.exp(scores - row_max)
    weights = (expons / lax.optimization_barrier(jnp.sum(expons, axis=2, keepdims=True))).astype(jnp.bfloat16)
    heads_out = jnp.einsum('hqk,khd->qhd', weights.astype(jnp.float32), value_three)
    heads_out = heads_out.astype(jnp.bfloat16).reshape(row_count, HEADS * HD)
    partial_value = jnp.dot(heads_out, weight_block, preferred_element_type=jnp.float32)
    section_out = (input_block.astype(jnp.float32) + partial_value).astype(jnp.bfloat16)
    wide_input = input_block.astype(jnp.float32)
    scale = lax.optimization_barrier(jnp.max(jnp.abs(wide_input), axis=1)) + 1e-06
    packed = (wide_input / scale[:, None]).astype(jnp.bfloat16)
    return (section_out, packed, scale)

def reference(query_heads, key_heads, value_heads, segment_ids, section_input, out_weight):
    section_out, packed, scale = lax.map(one_section, (query_heads, key_heads, value_heads, segment_ids, section_input, out_weight))
    received = jnp.concatenate([jnp.zeros_like(section_out[:1]), section_out[:-1]], axis=0)
    evicted = packed[::-1]
    evicted_scale = scale[::-1]
    return (received, evicted, evicted_scale)
```

```python
import functools
import math

import jax
import jax.numpy as jnp
from jax import lax
from jax.experimental import pallas as pl
from jax.experimental.pallas import tpu as pltpu
from jax.sharding import PartitionSpec as P

HD = 128
NEG = -1e30
MESH = pl.DeviceIdType.MESH


def kernel(
    dims,
    q_hbm, k_hbm, v_hbm, seg_ref, x_hbm, w_hbm,
    recv_hbm, ev_hbm, es_ref,
    q_v, k_v, v_v, x_v, w_v, heads, bias, part, send0, ring, ev_v, scale_v, zero_v,
    in_sem, w_sem, rs_send, rs_recv, fw_send, fw_recv, ev_send, ev_recv, ev_out_sem, zero_sem,
):
    sections, parts, rows, head_count, blocks, width, ev_blocks, ev_rows = dims
    total_rows = parts * rows
    p = lax.axis_index("pipe")
    y = lax.axis_index("tensor")
    d = lax.axis_index("dp")
    up = (p, lax.rem(y + 1, parts), d)
    down = (p, lax.rem(y + parts - 1, parts), d)
    ring_to = (up, down)
    mirror = (sections - 1 - p, y, d)
    after = (lax.rem(p + 1, sections), y, d)
    before = (lax.rem(p + sections - 1, sections), y, d)

    barrier = pltpu.get_barrier_semaphore()
    for device in (up, down, mirror, before):
        pl.semaphore_signal(barrier, inc=1, device_id=device, device_id_type=MESH)

    loads = []
    for i, (src, dst) in enumerate(((q_hbm, q_v), (k_hbm, k_v), (v_hbm, v_v))):
        copy = pltpu.make_async_copy(src.at[0], dst, in_sem.at[i])
        copy.start()
        loads.append(copy)

    def w_copy(side, j):
        cols = pl.ds(pl.multiple_of((side * blocks + j) * width, width), width)
        return pltpu.make_async_copy(w_hbm.at[0, :, cols], w_v.at[side, j], w_sem.at[side, j])

    def start_w(j, carry):
        w_copy(0, j).start()
        w_copy(1, j).start()
        return carry

    lax.fori_loop(0, blocks, start_w, 0)
    x_load = pltpu.make_async_copy(x_hbm.at[0], x_v, in_sem.at[3])
    x_load.start()

    chunk = (
        lax.rem(y + parts - 1, parts),
        lax.rem(y + 2, parts),
        y,
        lax.rem(y + 1, parts),
    )

    def attend(slot):
        start = pl.multiple_of(chunk[slot] * rows, rows)
        seg_all = seg_ref[...].astype(jnp.float32)
        seg_rows = seg_ref[:, pl.ds(start, rows)].astype(jnp.float32)
        seg_col = jnp.broadcast_to(seg_rows, (rows, rows)).T[:, :1]
        row_pos = lax.broadcasted_iota(jnp.int32, (rows, total_rows), 0) + start
        col_pos = lax.broadcasted_iota(jnp.int32, (rows, total_rows), 1)
        allowed = (seg_col == seg_all) & (col_pos <= row_pos)
        bias[...] = jnp.where(allowed, 0.0, NEG)

        def one_head(h, carry):
            cols = pl.ds(pl.multiple_of(h * HD, HD), HD)
            scores = lax.dot_general(
                q_v[pl.ds(start, rows), cols], k_v[:, cols],
                (((1,), (1,)), ((), ())), preferred_element_type=jnp.float32,
            )
            scores = scores * (math.log2(math.e) / math.sqrt(HD)) + bias[...]
            expons = jnp.exp2(scores - jnp.max(scores, axis=1, keepdims=True))
            inverse = 1.0 / jnp.sum(expons, axis=1, keepdims=True)
            weights = (expons * inverse).astype(jnp.bfloat16)
            out = jnp.dot(weights, v_v[:, cols], preferred_element_type=jnp.float32)
            heads[slot * rows:(slot + 1) * rows, cols] = out.astype(jnp.bfloat16)
            return carry

        lax.fori_loop(0, head_count, one_head, 0)

    def ring_copy(side, step, j):
        src = send0.at[side, j] if step == 0 else ring.at[side, step - 1, j]
        return pltpu.make_async_remote_copy(
            src_ref=src, dst_ref=ring.at[side, step, j],
            send_sem=rs_send.at[side, step, j], recv_sem=rs_recv.at[side, step, j],
            device_id=ring_to[side], device_id_type=MESH,
        )

    def first(side, j):
        slot = 0 if side == 0 else 3
        w_copy(side, j).wait()
        out = jnp.dot(
            heads[slot * rows:(slot + 1) * rows, :], w_v[side, j],
            preferred_element_type=jnp.float32,
        )
        send0[side, j] = out.astype(jnp.bfloat16)
        ring_copy(side, 0, j).start()

    def ev_copy(i):
        at = pl.ds(pl.multiple_of(i * ev_rows, ev_rows), ev_rows)
        return pltpu.make_async_remote_copy(
            src_ref=x_hbm.at[0, at, :], dst_ref=ev_v.at[i],
            send_sem=ev_send.at[i], recv_sem=ev_recv.at[i],
            device_id=mirror, device_id_type=MESH,
        )

    def ev_store(i):
        at = pl.ds(pl.multiple_of(i * ev_rows, ev_rows), ev_rows)
        return pltpu.make_async_copy(ev_v.at[i], ev_hbm.at[0, at, :], ev_out_sem.at[i])

    for copy in loads:
        copy.wait()
    attend(0)
    pl.semaphore_wait(barrier, 4)

    lead = 2

    def lead_step(j, carry):
        first(0, j)
        return carry

    lax.fori_loop(0, lead, lead_step, 0)

    def start_ev(i, carry):
        ev_copy(i).start()
        return carry

    lax.fori_loop(0, ev_blocks, start_ev, 0)
    attend(3)

    def first_step(j, carry):
        first(1, j)

        @pl.when(j + lead < blocks)
        def _():
            first(0, j + lead)

        return carry

    lax.fori_loop(0, blocks, first_step, 0)
    attend(1)
    attend(2)

    lo = ((0, 2 * rows, rows), (rows, 0, 2 * rows))

    def add_step(side, step, j):
        ring_copy(side, step, j).wait_recv()
        at = lo[side][step]
        total = ring[side, step, j].astype(jnp.float32) + part[side, j, at:at + rows, :]
        if step == 2:
            cols = pl.ds(pl.multiple_of((side * blocks + j) * width, width), width)
            total = total + x_v[:, cols].astype(jnp.float32)
        ring[side, step, j] = total.astype(jnp.bfloat16)

    def second_step(j, carry):
        for side in (0, 1):
            src = heads[rows:, :] if side == 0 else heads[:3 * rows, :]
            part[side, j] = jnp.dot(src, w_v[side, j], preferred_element_type=jnp.float32)
        for side in (0, 1):
            add_step(side, 0, j)
            ring_copy(side, 1, j).start()
        return carry

    lax.fori_loop(0, blocks, second_step, 0)

    def third_step(j, carry):
        for side in (0, 1):
            add_step(side, 1, j)
            ring_copy(side, 2, j).start()
        return carry

    lax.fori_loop(0, blocks, third_step, 0)
    x_load.wait()

    def out_cols(side, j):
        return pl.ds(pl.multiple_of((side * blocks + j) * width, width), width)

    def fw_copy(side, j):
        return pltpu.make_async_remote_copy(
            src_ref=ring.at[side, 2, j], dst_ref=recv_hbm.at[0, :, out_cols(side, j)],
            send_sem=fw_send.at[side, j], recv_sem=fw_recv.at[side, j],
            device_id=after, device_id_type=MESH,
        )

    def zero_copy(side, j):
        return pltpu.make_async_copy(zero_v, recv_hbm.at[0, :, out_cols(side, j)], zero_sem.at[side, j])

    @pl.when(p == 0)
    def _():
        zero_v[...] = jnp.zeros_like(zero_v)

        def start_zero(j, carry):
            for side in (0, 1):
                zero_copy(side, j).start()
            return carry

        lax.fori_loop(0, blocks, start_zero, 0)

    def evict(i):
        ev_copy(i).wait_recv()
        wide = ev_v[i].astype(jnp.float32)
        scale = jnp.max(jnp.abs(wide), axis=1, keepdims=True) + 1e-06
        ev_v[i] = (wide / scale).astype(jnp.bfloat16)
        at = pl.ds(pl.multiple_of(i * ev_rows, ev_rows), ev_rows)
        scale_v[at, :] = jnp.broadcast_to(scale, (ev_rows, HD))
        ev_store(i).start()

    def last_step(j, carry):
        for side in (0, 1):
            add_step(side, 2, j)

            @pl.when(p < sections - 1)
            def _():
                fw_copy(side, j).start()

        @pl.when(2 * j < ev_blocks)
        def _():
            evict(2 * j)
            evict(2 * j + 1)

        return carry

    lax.fori_loop(0, blocks, last_step, 0)
    es_ref[...] = scale_v[...].T[:1, :]

    def drain(j, carry):
        for side in (0, 1):
            for step in range(3):
                ring_copy(side, step, j).wait_send()

            @pl.when(p < sections - 1)
            def _():
                fw_copy(side, j).wait_send()

            @pl.when(p > 0)
            def _():
                fw_copy(side, j).wait_recv()

            @pl.when(p == 0)
            def _():
                zero_copy(side, j).wait()

        return carry

    lax.fori_loop(0, blocks, drain, 0)

    def drain_ev(i, carry):
        ev_copy(i).wait_send()
        ev_store(i).wait()
        return carry

    lax.fori_loop(0, ev_blocks, drain_ev, 0)


def solution(mesh):
    sections, parts = mesh.shape["pipe"], mesh.shape["tensor"]

    def per_device(query_heads, key_heads, value_heads, segment_ids, section_input, out_weight):
        total_rows, inner = query_heads.shape[1:]
        rows, features = section_input.shape[1:]
        blocks = 8
        width = features // (2 * blocks)
        ev_blocks = 8
        ev_rows = rows // ev_blocks
        dims = (sections, parts, rows, inner // HD, blocks, width, ev_blocks, ev_rows)
        bf16, f32 = jnp.bfloat16, jnp.float32
        any_spec = pl.BlockSpec(memory_space=pl.ANY)
        vmem_spec = pl.BlockSpec(memory_space=pltpu.VMEM)
        dma = pltpu.SemaphoreType.DMA
        return pl.pallas_call(
            functools.partial(kernel, dims),
            out_shape=(
                jax.ShapeDtypeStruct((1, rows, features), bf16),
                jax.ShapeDtypeStruct((1, rows, features), bf16),
                jax.ShapeDtypeStruct((1, rows), f32),
            ),
            in_specs=[any_spec, any_spec, any_spec, vmem_spec, any_spec, any_spec],
            out_specs=(any_spec, any_spec, vmem_spec),
            scratch_shapes=[
                pltpu.VMEM((total_rows, inner), bf16),
                pltpu.VMEM((total_rows, inner), bf16),
                pltpu.VMEM((total_rows, inner), bf16),
                pltpu.VMEM((rows, features), bf16),
                pltpu.VMEM((2, blocks, inner, width), bf16),
                pltpu.VMEM((total_rows, inner), bf16),
                pltpu.VMEM((rows, total_rows), f32),
                pltpu.VMEM((2, blocks, 3 * rows, width), f32),
                pltpu.VMEM((2, blocks, rows, width), bf16),
                pltpu.VMEM((2, 3, blocks, rows, width), bf16),
                pltpu.VMEM((ev_blocks, ev_rows, features), bf16),
                pltpu.VMEM((rows, HD), f32),
                pltpu.VMEM((rows, width), bf16),
                dma((4,)),
                dma((2, blocks)),
                dma((2, 3, blocks)),
                dma((2, 3, blocks)),
                dma((2, blocks)),
                dma((2, blocks)),
                dma((ev_blocks,)),
                dma((ev_blocks,)),
                dma((ev_blocks,)),
                dma((2, blocks)),
            ],
            compiler_params=pltpu.CompilerParams(
                collective_id=0, has_side_effects=True, vmem_limit_bytes=60 * 1024 * 1024
            ),
        )(query_heads, key_heads, value_heads, segment_ids, section_input, out_weight)

    return jax.shard_map(
        per_device,
        mesh=mesh,
        in_specs=(
            P(("dp", "pipe"), None, "tensor"),
            P(("dp", "pipe"), None, "tensor"),
            P(("dp", "pipe"), None, "tensor"),
            P(("dp", "pipe"), None),
            P(("dp", "pipe"), "tensor", None),
            P(("dp", "pipe"), "tensor", None),
        ),
        out_specs=(
            P(("dp", "pipe"), "tensor", None),
            P(("dp", "pipe"), "tensor", None),
            P(("dp", "pipe"), "tensor"),
        ),
        check_vma=False,
    )
```

```python
import functools
import math

import jax
import jax.numpy as jnp
from jax import lax
from jax.experimental import pallas as pl
from jax.experimental.pallas import tpu as pltpu
from jax.sharding import PartitionSpec as P

HD = 128
NEG = -1e30
MESH = pl.DeviceIdType.MESH
UNROLL = 4


def kernel(
    dims,
    q_hbm, k_hbm, v_hbm, seg_ref, x_hbm, w_hbm,
    recv_out, ev_out, es_ref,
    q_v, k_v, v_v, x_v, w_v, heads, seg_t, bias, part, send0, ring, ev_v, scale_v, zero_v,
    in_sem, w_sem, rs_send, rs_recv, fw_send, fw_recv, ev_send, ev_recv, ev_out_sem, zero_sem,
):
    sections, parts, rows, head_count, blocks, width, ev_blocks, ev_rows = dims
    total_rows = parts * rows
    p = lax.axis_index("pipe")
    y = lax.axis_index("tensor")
    d = lax.axis_index("dp")
    up = (p, lax.rem(y + 1, parts), d)
    down = (p, lax.rem(y + parts - 1, parts), d)
    ring_to = (up, down)
    mirror = (sections - 1 - p, y, d)
    after = (lax.rem(p + 1, sections), y, d)
    before = (lax.rem(p + sections - 1, sections), y, d)

    barrier = pltpu.get_barrier_semaphore()
    for device in (up, down, mirror, before):
        pl.semaphore_signal(barrier, inc=1, device_id=device, device_id_type=MESH)

    chunk = (
        lax.rem(y + parts - 1, parts),
        lax.rem(y + 2, parts),
        y,
        lax.rem(y + 1, parts),
    )
    pairs = ((0, 3), (1, 2))
    group = head_count // 2

    def rows_at(slot):
        return pl.multiple_of(chunk[slot] * rows, rows)

    def q_copy(pair, i):
        slot = pairs[pair][i]
        return pltpu.make_async_copy(
            q_hbm.at[0, pl.ds(rows_at(slot), rows), :],
            q_v.at[pair, pl.ds(i * rows, rows), :],
            in_sem.at[2 * pair + i],
        )

    def kv_copy(i, part_of):
        src, dst = ((k_hbm, k_v), (v_hbm, v_v))[i]
        cols = pl.ds(part_of * group * HD, group * HD)
        return pltpu.make_async_copy(
            src.at[0, :, cols], dst.at[:, cols], in_sem.at[4 + 2 * part_of + i]
        )

    x_load = pltpu.make_async_copy(x_hbm.at[0], x_v, in_sem.at[8])

    def w_copy(side, j):
        cols = pl.ds(pl.multiple_of((side * blocks + j) * width, width), width)
        return pltpu.make_async_copy(w_hbm.at[0, :, cols], w_v.at[side, j], w_sem.at[side, j])

    for i in (0, 1):
        q_copy(0, i).start()
    for part_of in (0, 1):
        for i in (0, 1):
            kv_copy(i, part_of).start()

    seg_all = seg_ref[...].astype(jnp.float32)
    seg_t[...] = jnp.broadcast_to(seg_all, (rows, total_rows)).T

    def set_bias(pair):
        for i in (0, 1):
            start = rows_at(pairs[pair][i])
            seg_rows = seg_ref[:, pl.ds(start, rows)].astype(jnp.float32)
            key_pos = lax.broadcasted_iota(jnp.int32, (total_rows, rows), 0)
            row_pos = lax.broadcasted_iota(jnp.int32, (total_rows, rows), 1) + start
            allowed = (seg_t[...] == seg_rows) & (key_pos <= row_pos)
            bias[:, i * rows:(i + 1) * rows] = jnp.where(allowed, 0.0, NEG)

    def attend(pair, first_head, count):
        def some_heads(i, carry):
            for u in range(UNROLL):
                h = first_head + i * UNROLL + u
                cols = pl.ds(pl.multiple_of(h * HD, HD), HD)
                scores = lax.dot_general(
                    k_v[:, cols], q_v[pair, :, cols],
                    (((1,), (1,)), ((), ())), preferred_element_type=jnp.float32,
                )
                scores = scores * (math.log2(math.e) / math.sqrt(HD)) + bias[...]
                expons = jnp.exp2(scores - jnp.max(scores, axis=0, keepdims=True))
                inverse = 1.0 / jnp.sum(expons, axis=0, keepdims=True)
                weights = (expons * inverse).astype(jnp.bfloat16)
                out = lax.dot_general(
                    weights, v_v[:, cols],
                    (((0,), (0,)), ((), ())), preferred_element_type=jnp.float32,
                ).astype(jnp.bfloat16)
                for i_slot in (0, 1):
                    at = pairs[pair][i_slot] * rows
                    heads[at:at + rows, cols] = out[i_slot * rows:(i_slot + 1) * rows]
            return carry

        lax.fori_loop(0, count // UNROLL, some_heads, 0)

    def ring_copy(side, step, j):
        src = send0.at[side, j] if step == 0 else ring.at[side, step - 1, j]
        return pltpu.make_async_remote_copy(
            src_ref=src, dst_ref=ring.at[side, step, j],
            send_sem=rs_send.at[side, step, j], recv_sem=rs_recv.at[side, step, j],
            device_id=ring_to[side], device_id_type=MESH,
        )

    def first(side, j):
        slot = 0 if side == 0 else 3
        w_copy(side, j).wait()
        out = jnp.dot(
            heads[slot * rows:(slot + 1) * rows, :], w_v[side, j],
            preferred_element_type=jnp.float32,
        )
        send0[side, j] = out.astype(jnp.bfloat16)
        ring_copy(side, 0, j).start()

    def ev_copy(i):
        at = pl.ds(pl.multiple_of(i * ev_rows, ev_rows), ev_rows)
        return pltpu.make_async_remote_copy(
            src_ref=x_hbm.at[0, at, :], dst_ref=ev_v.at[i],
            send_sem=ev_send.at[i], recv_sem=ev_recv.at[i],
            device_id=mirror, device_id_type=MESH,
        )

    def ev_store(i):
        at = pl.ds(pl.multiple_of(i * ev_rows, ev_rows), ev_rows)
        return pltpu.make_async_copy(ev_v.at[i], ev_out.at[0, at, :], ev_out_sem.at[i])

    def start_w(j, carry):
        w_copy(0, j).start()
        w_copy(1, j).start()
        return carry

    set_bias(0)
    for i in (0, 1):
        q_copy(0, i).wait()
        kv_copy(i, 0).wait()
    attend(0, 0, group)
    for i in (0, 1):
        kv_copy(i, 1).wait()
    lax.fori_loop(0, blocks, start_w, 0)
    for i in (0, 1):
        q_copy(1, i).start()
    x_load.start()
    attend(0, group, group)
    pl.semaphore_wait(barrier, 4)

    def first_step(j, carry):
        first(0, j)
        first(1, j)

        @pl.when(j < ev_blocks)
        def _():
            ev_copy(j).start()

        return carry

    lax.fori_loop(0, blocks, first_step, 0)
    set_bias(1)
    for i in (0, 1):
        q_copy(1, i).wait()
    attend(1, 0, head_count)

    lo = ((0, 2 * rows, rows), (rows, 0, 2 * rows))

    def add_step(side, step, j):
        ring_copy(side, step, j).wait_recv()
        at = lo[side][step]
        total = ring[side, step, j].astype(jnp.float32) + part[side, j, at:at + rows, :]
        if step == 2:
            cols = pl.ds(pl.multiple_of((side * blocks + j) * width, width), width)
            total = total + x_v[:, cols].astype(jnp.float32)
        ring[side, step, j] = total.astype(jnp.bfloat16)

    def second_step(j, carry):
        for side in (0, 1):
            src = heads[rows:, :] if side == 0 else heads[:3 * rows, :]
            part[side, j] = jnp.dot(src, w_v[side, j], preferred_element_type=jnp.float32)
        for side in (0, 1):
            add_step(side, 0, j)
            ring_copy(side, 1, j).start()
        return carry

    lax.fori_loop(0, blocks, second_step, 0)

    def third_step(j, carry):
        for side in (0, 1):
            add_step(side, 1, j)
            ring_copy(side, 2, j).start()
        return carry

    lax.fori_loop(0, blocks, third_step, 0)
    x_load.wait()

    def out_cols(side, j):
        return pl.ds(pl.multiple_of((side * blocks + j) * width, width), width)

    def fw_copy(side, j):
        return pltpu.make_async_remote_copy(
            src_ref=ring.at[side, 2, j], dst_ref=recv_out.at[0, :, out_cols(side, j)],
            send_sem=fw_send.at[side, j], recv_sem=fw_recv.at[side, j],
            device_id=after, device_id_type=MESH,
        )

    def zero_copy(side, j):
        return pltpu.make_async_copy(zero_v, recv_out.at[0, :, out_cols(side, j)], zero_sem.at[side, j])

    @pl.when(p == 0)
    def _():
        zero_v[...] = jnp.zeros_like(zero_v)

        def start_zero(j, carry):
            for side in (0, 1):
                zero_copy(side, j).start()
            return carry

        lax.fori_loop(0, blocks, start_zero, 0)

    def evict(i):
        ev_copy(i).wait_recv()
        wide = ev_v[i].astype(jnp.float32)
        scale = jnp.max(jnp.abs(wide), axis=1, keepdims=True) + 1e-06
        ev_v[i] = (wide / scale).astype(jnp.bfloat16)
        at = pl.ds(pl.multiple_of(i * ev_rows, ev_rows), ev_rows)
        scale_v[at, :] = jnp.broadcast_to(scale, (ev_rows, HD))
        ev_store(i).start()

    def last_step(j, carry):
        for side in (0, 1):
            add_step(side, 2, j)

            @pl.when(p < sections - 1)
            def _():
                fw_copy(side, j).start()

        @pl.when(2 * j < ev_blocks)
        def _():
            evict(2 * j)
            evict(2 * j + 1)

        return carry

    lax.fori_loop(0, blocks, last_step, 0)
    es_ref[...] = scale_v[...].T[:1, :]

    def drain(j, carry):
        for side in (0, 1):
            for step in range(3):
                ring_copy(side, step, j).wait_send()

            @pl.when(p < sections - 1)
            def _():
                fw_copy(side, j).wait_send()

            @pl.when(p > 0)
            def _():
                fw_copy(side, j).wait_recv()

            @pl.when(p == 0)
            def _():
                zero_copy(side, j).wait()

        return carry

    lax.fori_loop(0, blocks, drain, 0)

    def drain_ev(i, carry):
        ev_copy(i).wait_send()
        ev_store(i).wait()
        return carry

    lax.fori_loop(0, ev_blocks, drain_ev, 0)


def finish(*refs):
    srcs, dsts, sems = refs[:3], refs[3:6], refs[6]
    copies = [
        pltpu.make_async_copy(src, dst, sems.at[i]) for i, (src, dst) in enumerate(zip(srcs, dsts))
    ]
    for copy in copies:
        copy.start()
    for copy in copies:
        copy.wait()


def solution(mesh):
    sections, parts = mesh.shape["pipe"], mesh.shape["tensor"]

    def per_device(*args):
        args = [pltpu.with_memory_space_constraint(a, pltpu.HBM) for a in args]
        total_rows, inner = args[0].shape[1:]
        rows, features = args[4].shape[1:]
        blocks = 8
        width = features // (2 * blocks)
        ev_blocks = 8
        ev_rows = rows // ev_blocks
        dims = (sections, parts, rows, inner // HD, blocks, width, ev_blocks, ev_rows)
        bf16, f32 = jnp.bfloat16, jnp.float32
        any_spec = pl.BlockSpec(memory_space=pl.ANY)
        vmem_spec = pl.BlockSpec(memory_space=pltpu.VMEM)
        dma = pltpu.SemaphoreType.DMA
        shapes = (
            jax.ShapeDtypeStruct((1, rows, features), bf16),
            jax.ShapeDtypeStruct((1, rows, features), bf16),
            jax.ShapeDtypeStruct((1, rows), f32),
        )
        outs = pl.pallas_call(
            functools.partial(kernel, dims),
            out_shape=shapes,
            in_specs=[any_spec, any_spec, any_spec, vmem_spec, any_spec, any_spec],
            out_specs=(any_spec, any_spec, vmem_spec),
            scratch_shapes=[
                pltpu.VMEM((2, 2 * rows, inner), bf16),
                pltpu.VMEM((total_rows, inner), bf16),
                pltpu.VMEM((total_rows, inner), bf16),
                pltpu.VMEM((rows, features), bf16),
                pltpu.VMEM((2, blocks, inner, width), bf16),
                pltpu.VMEM((total_rows, inner), bf16),
                pltpu.VMEM((total_rows, rows), f32),
                pltpu.VMEM((total_rows, 2 * rows), f32),
                pltpu.VMEM((2, blocks, 3 * rows, width), f32),
                pltpu.VMEM((2, blocks, rows, width), bf16),
                pltpu.VMEM((2, 3, blocks, rows, width), bf16),
                pltpu.VMEM((ev_blocks, ev_rows, features), bf16),
                pltpu.VMEM((rows, HD), f32),
                pltpu.VMEM((rows, width), bf16),
                dma((9,)),
                dma((2, blocks)),
                dma((2, 3, blocks)),
                dma((2, 3, blocks)),
                dma((2, blocks)),
                dma((2, blocks)),
                dma((ev_blocks,)),
                dma((ev_blocks,)),
                dma((ev_blocks,)),
                dma((2, blocks)),
            ],
            compiler_params=pltpu.CompilerParams(
                collective_id=0, has_side_effects=True, vmem_limit_bytes=47 * 1024 * 1024
            ),
        )(*args)
        return pl.pallas_call(
            finish,
            out_shape=shapes,
            in_specs=[vmem_spec] * 3,
            out_specs=(any_spec,) * 3,
            scratch_shapes=[dma((3,))],
            compiler_params=pltpu.CompilerParams(vmem_limit_bytes=8 * 1024 * 1024),
        )(*outs)

    return jax.shard_map(
        per_device,
        mesh=mesh,
        in_specs=(
            P(("dp", "pipe"), None, "tensor"),
            P(("dp", "pipe"), None, "tensor"),
            P(("dp", "pipe"), None, "tensor"),
            P(("dp", "pipe"), None),
            P(("dp", "pipe"), "tensor", None),
            P(("dp", "pipe"), "tensor", None),
        ),
        out_specs=(
            P(("dp", "pipe"), "tensor", None),
            P(("dp", "pipe"), "tensor", None),
            P(("dp", "pipe"), "tensor"),
        ),
        check_vma=False,
    )
```

```python
import functools
import math

import jax
import jax.numpy as jnp
from jax import lax
from jax.experimental import pallas as pl
from jax.experimental.pallas import tpu as pltpu
from jax.sharding import PartitionSpec as P

HD = 128
NEG = -1e30
MESH = pl.DeviceIdType.MESH
UNROLL = 4
CUTS = 4


def kernel(
    dims,
    q_hbm, k_hbm, v_hbm, seg_ref, x_hbm, w_hbm,
    recv_out, ev_out, es_ref,
    q_v, k_v, v_v, x_v, w_v, heads, seg_t, bias, part, send0, ring, ev_v, scale_v, zero_v,
    in_sem, w_sem, rs_send, rs_recv, fw_send, fw_recv, ev_send, ev_recv, ev_out_sem, zero_sem,
):
    sections, parts, rows, head_count, blocks, width, ev_blocks, ev_rows = dims
    total_rows = parts * rows
    p = lax.axis_index("pipe")
    y = lax.axis_index("tensor")
    d = lax.axis_index("dp")
    up = (p, lax.rem(y + 1, parts), d)
    down = (p, lax.rem(y + parts - 1, parts), d)
    ring_to = (up, down)
    mirror = (sections - 1 - p, y, d)
    after = (lax.rem(p + 1, sections), y, d)
    before = (lax.rem(p + sections - 1, sections), y, d)

    barrier = pltpu.get_barrier_semaphore()
    for device in (up, down, mirror, before):
        pl.semaphore_signal(barrier, inc=1, device_id=device, device_id_type=MESH)

    chunk = (
        lax.rem(y + parts - 1, parts),
        lax.rem(y + 2, parts),
        y,
        lax.rem(y + 1, parts),
    )
    pairs = ((0, 3), (1, 2))
    group = head_count // 2

    def rows_at(slot):
        return pl.multiple_of(chunk[slot] * rows, rows)

    def q_copy(pair, i):
        slot = pairs[pair][i]
        return pltpu.make_async_copy(
            q_hbm.at[0, pl.ds(rows_at(slot), rows), :],
            q_v.at[pair, pl.ds(i * rows, rows), :],
            in_sem.at[2 * pair + i],
        )

    def kv_copy(i, part_of):
        src, dst = ((k_hbm, k_v), (v_hbm, v_v))[i]
        cols = pl.ds(part_of * group * HD, group * HD)
        return pltpu.make_async_copy(
            src.at[0, :, cols], dst.at[:, cols], in_sem.at[4 + 2 * part_of + i]
        )

    x_load = pltpu.make_async_copy(x_hbm.at[0], x_v, in_sem.at[8])

    def w_copy(side, j):
        cols = pl.ds(pl.multiple_of((side * blocks + j) * width, width), width)
        return pltpu.make_async_copy(w_hbm.at[0, :, cols], w_v.at[side, j], w_sem.at[side, j])

    for i in (0, 1):
        q_copy(0, i).start()
    for part_of in (0, 1):
        for i in (0, 1):
            kv_copy(i, part_of).start()

    seg_all = seg_ref[...].astype(jnp.float32)
    seg_t[...] = jnp.broadcast_to(seg_all, (rows, total_rows)).T

    def set_bias(pair):
        for i in (0, 1):
            start = rows_at(pairs[pair][i])
            seg_rows = seg_ref[:, pl.ds(start, rows)].astype(jnp.float32)
            key_pos = lax.broadcasted_iota(jnp.int32, (total_rows, rows), 0)
            row_pos = lax.broadcasted_iota(jnp.int32, (total_rows, rows), 1) + start
            allowed = (seg_t[...] == seg_rows) & (key_pos <= row_pos)
            bias[:, i * rows:(i + 1) * rows] = jnp.where(allowed, 0.0, NEG)

    def attend(pair, first_head, count):
        def some_heads(i, carry):
            for u in range(UNROLL):
                h = first_head + i * UNROLL + u
                cols = pl.ds(pl.multiple_of(h * HD, HD), HD)
                scores = lax.dot_general(
                    k_v[:, cols], q_v[pair, :, cols],
                    (((1,), (1,)), ((), ())), preferred_element_type=jnp.float32,
                )
                scores = scores * (math.log2(math.e) / math.sqrt(HD)) + bias[...]
                expons = jnp.exp2(scores - jnp.max(scores, axis=0, keepdims=True))
                inverse = 1.0 / jnp.sum(expons, axis=0, keepdims=True)
                weights = (expons * inverse).astype(jnp.bfloat16)
                out = lax.dot_general(
                    weights, v_v[:, cols],
                    (((0,), (0,)), ((), ())), preferred_element_type=jnp.float32,
                ).astype(jnp.bfloat16)
                for i_slot in (0, 1):
                    at = pairs[pair][i_slot] * rows
                    heads[at:at + rows, cols] = out[i_slot * rows:(i_slot + 1) * rows]
            return carry

        lax.fori_loop(0, count // UNROLL, some_heads, 0)

    def ring_copy(side, step, j):
        src = send0.at[side, j] if step == 0 else ring.at[side, step - 1, j]
        return pltpu.make_async_remote_copy(
            src_ref=src, dst_ref=ring.at[side, step, j],
            send_sem=rs_send.at[side, step, j], recv_sem=rs_recv.at[side, step, j],
            device_id=ring_to[side], device_id_type=MESH,
        )

    def first(side, j):
        slot = 0 if side == 0 else 3
        w_copy(side, j).wait()
        out = jnp.dot(
            heads[slot * rows:(slot + 1) * rows, :], w_v[side, j],
            preferred_element_type=jnp.float32,
        )
        send0[side, j] = out.astype(jnp.bfloat16)
        ring_copy(side, 0, j).start()

    def ev_copy(i):
        at = pl.ds(pl.multiple_of(i * ev_rows, ev_rows), ev_rows)
        return pltpu.make_async_remote_copy(
            src_ref=x_hbm.at[0, at, :], dst_ref=ev_v.at[i],
            send_sem=ev_send.at[i], recv_sem=ev_recv.at[i],
            device_id=mirror, device_id_type=MESH,
        )

    def ev_store(i):
        at = pl.ds(pl.multiple_of(i * ev_rows, ev_rows), ev_rows)
        return pltpu.make_async_copy(ev_v.at[i], ev_out.at[0, at, :], ev_out_sem.at[i])

    def start_w(j, carry):
        w_copy(0, j).start()
        w_copy(1, j).start()
        return carry

    set_bias(0)
    for i in (0, 1):
        q_copy(0, i).wait()
        kv_copy(i, 0).wait()
    attend(0, 0, group)
    for i in (0, 1):
        kv_copy(i, 1).wait()
    lax.fori_loop(0, blocks, start_w, 0)
    for i in (0, 1):
        q_copy(1, i).start()
    x_load.start()
    attend(0, group, group)
    pl.semaphore_wait(barrier, 4)

    def first_step(j, carry):
        first(0, j)
        first(1, j)

        @pl.when(j < ev_blocks)
        def _():
            ev_copy(j).start()

        return carry

    lax.fori_loop(0, blocks, first_step, 0)
    set_bias(1)
    for i in (0, 1):
        q_copy(1, i).wait()
    attend(1, 0, head_count)

    lo = ((0, 2 * rows, rows), (rows, 0, 2 * rows))

    def add_step(side, step, j):
        ring_copy(side, step, j).wait_recv()
        at = lo[side][step]
        total = ring[side, step, j].astype(jnp.float32) + part[side, j, at:at + rows, :]
        if step == 2:
            cols = pl.ds(pl.multiple_of((side * blocks + j) * width, width), width)
            total = total + x_v[:, cols].astype(jnp.float32)
        ring[side, step, j] = total.astype(jnp.bfloat16)

    def second_step(j, carry):
        for side in (0, 1):
            src = heads[rows:, :] if side == 0 else heads[:3 * rows, :]
            part[side, j] = jnp.dot(src, w_v[side, j], preferred_element_type=jnp.float32)
        for side in (0, 1):
            add_step(side, 0, j)
            ring_copy(side, 1, j).start()
        return carry

    lax.fori_loop(0, blocks, second_step, 0)

    def third_step(j, carry):
        for side in (0, 1):
            add_step(side, 1, j)
            ring_copy(side, 2, j).start()
        return carry

    lax.fori_loop(0, blocks, third_step, 0)
    x_load.wait()

    def out_cols(side, j):
        return pl.ds(pl.multiple_of((side * blocks + j) * width, width), width)

    def fw_copy(side, j):
        return pltpu.make_async_remote_copy(
            src_ref=ring.at[side, 2, j], dst_ref=recv_out.at[0, :, out_cols(side, j)],
            send_sem=fw_send.at[side, j], recv_sem=fw_recv.at[side, j],
            device_id=after, device_id_type=MESH,
        )

    def zero_copy(side, j):
        return pltpu.make_async_copy(zero_v, recv_out.at[0, :, out_cols(side, j)], zero_sem.at[side, j])

    @pl.when(p == 0)
    def _():
        zero_v[...] = jnp.zeros_like(zero_v)

        def start_zero(j, carry):
            for side in (0, 1):
                zero_copy(side, j).start()
            return carry

        lax.fori_loop(0, blocks, start_zero, 0)

    def evict(i):
        ev_copy(i).wait_recv()
        wide = ev_v[i].astype(jnp.float32)
        scale = jnp.max(jnp.abs(wide), axis=1, keepdims=True) + 1e-06
        ev_v[i] = (wide / scale).astype(jnp.bfloat16)
        at = pl.ds(pl.multiple_of(i * ev_rows, ev_rows), ev_rows)
        scale_v[at, :] = jnp.broadcast_to(scale, (ev_rows, HD))
        ev_store(i).start()

    def last_step(j, carry):
        for side in (0, 1):
            add_step(side, 2, j)

            @pl.when(p < sections - 1)
            def _():
                fw_copy(side, j).start()

        @pl.when(2 * j < ev_blocks)
        def _():
            evict(2 * j)
            evict(2 * j + 1)

        return carry

    lax.fori_loop(0, blocks, last_step, 0)
    es_ref[...] = scale_v[...].T[:1, :]

    def drain(j, carry):
        for side in (0, 1):
            for step in range(3):
                ring_copy(side, step, j).wait_send()

            @pl.when(p < sections - 1)
            def _():
                fw_copy(side, j).wait_send()

            @pl.when(p > 0)
            def _():
                fw_copy(side, j).wait_recv()

            @pl.when(p == 0)
            def _():
                zero_copy(side, j).wait()

        return carry

    lax.fori_loop(0, blocks, drain, 0)

    def drain_ev(i, carry):
        ev_copy(i).wait_send()
        ev_store(i).wait()
        return carry

    lax.fori_loop(0, ev_blocks, drain_ev, 0)


def finish(recv_ref, ev_ref, scale_ref, recv_hbm, ev_hbm, scale_hbm, sems):
    step = recv_ref.shape[1] // CUTS
    copies = [pltpu.make_async_copy(scale_ref, scale_hbm, sems.at[2 * CUTS])]
    for i in range(CUTS):
        at = pl.ds(i * step, step)
        for n, (src, dst) in enumerate(((recv_ref, recv_hbm), (ev_ref, ev_hbm))):
            copies.append(
                pltpu.make_async_copy(src.at[0, at, :], dst.at[0, at, :], sems.at[2 * i + n])
            )
    for copy in copies:
        copy.start()
    for copy in copies:
        copy.wait()


def solution(mesh):
    sections, parts = mesh.shape["pipe"], mesh.shape["tensor"]

    def per_device(*args):
        args = [pltpu.with_memory_space_constraint(a, pltpu.HBM) for a in args]
        total_rows, inner = args[0].shape[1:]
        rows, features = args[4].shape[1:]
        blocks = 8
        width = features // (2 * blocks)
        ev_blocks = 8
        ev_rows = rows // ev_blocks
        dims = (sections, parts, rows, inner // HD, blocks, width, ev_blocks, ev_rows)
        bf16, f32 = jnp.bfloat16, jnp.float32
        any_spec = pl.BlockSpec(memory_space=pl.ANY)
        vmem_spec = pl.BlockSpec(memory_space=pltpu.VMEM)
        dma = pltpu.SemaphoreType.DMA
        shapes = (
            jax.ShapeDtypeStruct((1, rows, features), bf16),
            jax.ShapeDtypeStruct((1, rows, features), bf16),
            jax.ShapeDtypeStruct((1, rows), f32),
        )
        outs = pl.pallas_call(
            functools.partial(kernel, dims),
            out_shape=shapes,
            in_specs=[any_spec, any_spec, any_spec, vmem_spec, any_spec, any_spec],
            out_specs=(any_spec, any_spec, vmem_spec),
            scratch_shapes=[
                pltpu.VMEM((2, 2 * rows, inner), bf16),
                pltpu.VMEM((total_rows, inner), bf16),
                pltpu.VMEM((total_rows, inner), bf16),
                pltpu.VMEM((rows, features), bf16),
                pltpu.VMEM((2, blocks, inner, width), bf16),
                pltpu.VMEM((total_rows, inner), bf16),
                pltpu.VMEM((total_rows, rows), f32),
                pltpu.VMEM((total_rows, 2 * rows), f32),
                pltpu.VMEM((2, blocks, 3 * rows, width), f32),
                pltpu.VMEM((2, blocks, rows, width), bf16),
                pltpu.VMEM((2, 3, blocks, rows, width), bf16),
                pltpu.VMEM((ev_blocks, ev_rows, features), bf16),
                pltpu.VMEM((rows, HD), f32),
                pltpu.VMEM((rows, width), bf16),
                dma((9,)),
                dma((2, blocks)),
                dma((2, 3, blocks)),
                dma((2, 3, blocks)),
                dma((2, blocks)),
                dma((2, blocks)),
                dma((ev_blocks,)),
                dma((ev_blocks,)),
                dma((ev_blocks,)),
                dma((2, blocks)),
            ],
            compiler_params=pltpu.CompilerParams(
                collective_id=0, has_side_effects=True, vmem_limit_bytes=47 * 1024 * 1024
            ),
        )(*args)
        return pl.pallas_call(
            finish,
            out_shape=shapes,
            in_specs=[vmem_spec] * 3,
            out_specs=(any_spec,) * 3,
            scratch_shapes=[dma((2 * CUTS + 1,))],
            compiler_params=pltpu.CompilerParams(vmem_limit_bytes=8 * 1024 * 1024),
        )(*outs)

    return jax.shard_map(
        per_device,
        mesh=mesh,
        in_specs=(
            P(("dp", "pipe"), None, "tensor"),
            P(("dp", "pipe"), None, "tensor"),
            P(("dp", "pipe"), None, "tensor"),
            P(("dp", "pipe"), None),
            P(("dp", "pipe"), "tensor", None),
            P(("dp", "pipe"), "tensor", None),
        ),
        out_specs=(
            P(("dp", "pipe"), "tensor", None),
            P(("dp", "pipe"), "tensor", None),
            P(("dp", "pipe"), "tensor"),
        ),
        check_vma=False,
    )
```
